128 devices in a mesh: pairs: 16 (over z, x), days: 8 (over y, core).
Axes of the slice: x: 4, y: 4, z: 4, core: 2. Of those that a mesh axis runs over, the one named last changes fastest.
Arguments:
- spectra: bfloat16 [8, 512, 2048], P('days', None, 'pairs'), may hold values from -6 to 6
- observed: bfloat16 [32, 64, 64, 128], P('pairs'), may hold values from -6 to 6
- pair_blocks: int32 [32, 2], replicated, may hold values from 0 to 7, as said below
- members: int32 [512], replicated, may hold values from 0 to 511, each once
- day_mask: int32 [32, 8], P('pairs'), may hold values from 0 to 1, as said below
Outputs:
- adjoint_spectra: float32 [8, 512, 2048], P('days', None, 'pairs')
The draws below stay inside these ranges and needn't reach their ends.
Inputs may be any that keep to these rules, and one draw needn't show every extreme that they name: `pair_blocks`: each row holds two station block numbers, the first not above the second; no two rows are alike. `members`: every station appears once. `day_mask`: every listed pair is used on at least one day.
All inputs are finite; a program needn't handle non-finite values.
Results may differ from the reference program's by a relative error of at most 0.0025.
Values may be sent and summed in bfloat16 or wider, within the bound.
A program may use at most 64 MiB of HBM per device.

```python
import math
import jax
import jax.numpy as jnp
import numpy as np
from jax import lax

B = 64
NSTA = 512
F = 1024
L = 128
NBLK = 8
NPAIRS = 32
DAYS = 8


def draw_pair_blocks(key, part):
    upper_rows, upper_cols = np.triu_indices(NBLK)
    chosen = jax.random.permutation(key, upper_rows.shape[0])[:NPAIRS]
    left_blocks = jnp.asarray(upper_rows, jnp.int32)[chosen]
    right_blocks = jnp.asarray(upper_cols, jnp.int32)[chosen]
    return jnp.stack([left_blocks, right_blocks], axis=1).astype(jnp.int32)


def draw_day_mask(key, part):
    key_bits, key_pick = jax.random.split(jax.random.fold_in(key, 17))
    coin_draws = jax.random.randint(key_bits, (NPAIRS, DAYS), 0, 4)
    forced = jax.random.randint(key_pick, (NPAIRS,), 0, DAYS)
    picked = jnp.arange(DAYS, dtype=jnp.int32)[None, :] == forced[:, None]
    return jnp.where((coin_draws < 3) | picked, 1, 0).astype(jnp.int32)


def level_of(key, shape, pieces, low, largest):
    def one(axis_at, shards_of):
        draws = jax.random.uniform(jax.random.fold_in(jax.random.fold_in(key, 6), axis_at), (shards_of,), jnp.float32, low / len(pieces), largest / len(pieces))
        return jnp.repeat(jnp.exp(draws), shape[axis_at] // shards_of).reshape((-1,) + (1,) * (len(shape) - axis_at - 1))

    level = one(*pieces[0])
    for cut in pieces[1:]:
        level = level * one(*cut)
    return level


def normal_values(own_key, extent, scale, reach, pieces=(), kind=jnp.bfloat16):
    result = scale * jax.random.normal(own_key, extent, jnp.float32)
    if pieces:
        result = result * level_of(own_key, extent, pieces, -0.22, 0.18)
    return jnp.clip(result, -reach, reach).astype(kind)


def setup_inputs(seed: int = 0) -> dict:
    streams_of = jax.random.split(jax.random.key(seed), 6)
    return {
        "spectra": normal_values(streams_of[0], (DAYS, NSTA, 2 * F), 1.0, 6.0, ((0, 8), (2, 16))),
        "observed": normal_values(streams_of[1], (NPAIRS, B, B, L), 1.0, 6.0, ((0, 16),)),
        "pair_blocks": draw_pair_blocks(jax.random.fold_in(streams_of[5], 71), 0),
        "members": jax.random.permutation(streams_of[3], NSTA).astype(jnp.int32),
        "day_mask": draw_day_mask(jax.random.fold_in(streams_of[5], 71), 0),
    }


def dft_tables():
    column = jnp.arange(2 * F, dtype=jnp.int32)
    frequency = column // 128 * 64 + column % 64
    part_of = column % 128 // 64
    lag_of = jnp.arange(L, dtype=jnp.int32) - L // 2
    phase_idx = frequency[:, None] * lag_of[None, :] % (2 * F)
    angles = jnp.float32(math.pi) * phase_idx.astype(jnp.float32) / F
    norm_scale = 1.0 / math.sqrt(F)
    cosine = jnp.cos(angles) * norm_scale
    sine_part = jnp.sin(angles) * norm_scale
    forward = jnp.where(part_of[:, None] == 0, cosine, -sine_part).astype(jnp.bfloat16)
    backward = jnp.where(part_of[:, None] == 0, cosine, sine_part).T.astype(jnp.bfloat16)
    return (forward, backward)

def hilbert_table():
    lag_rows = jnp.arange(L, dtype=jnp.int32)[:, None]
    lag_cols = jnp.arange(L, dtype=jnp.int32)[None, :]
    offset = (lag_cols - lag_rows) % L
    is_odd = offset % 2 == 1
    angles = jnp.float32(math.pi) * offset.astype(jnp.float32) / L
    safe_sin = jnp.where(is_odd, jnp.sin(angles), jnp.float32(1.0))
    return jnp.where(is_odd, 2.0 / L * jnp.cos(angles) / safe_sin, jnp.float32(0.0)).astype(jnp.float32)

def split_tiles(spec_array):
    shaped = spec_array.reshape(spec_array.shape[:-1] + (F // 64, 2, 64))
    return (shaped[..., 0, :], shaped[..., 1, :])

def join_tiles(real_part, imag_part):
    joined = jnp.stack([real_part, imag_part], axis=-2)
    return joined.reshape(joined.shape[:-3] + (2 * F,))

def weighted_residual(stacked, observed_f, hilbert):
    flat_s = stacked.reshape(-1, L)
    flat_o = observed_f.reshape(-1, L)
    hil_s = jnp.dot(flat_s, hilbert, precision=lax.Precision.HIGHEST, preferred_element_type=jnp.float32)
    hil_o = jnp.dot(flat_o, hilbert, precision=lax.Precision.HIGHEST, preferred_element_type=jnp.float32)
    env_s = jnp.sqrt(flat_s * flat_s + hil_s * hil_s)
    env_o = jnp.sqrt(flat_o * flat_o + hil_o * hil_o)
    weight = (1.0 + env_s) / (1.0 + env_s + env_o)
    return ((flat_s - flat_o) * weight).reshape(stacked.shape)

def reference(spectra, observed, pair_blocks, members, day_mask):
    forward, backward = dft_tables()
    backward_f = backward.astype(jnp.float32)
    hilbert = hilbert_table()
    offsets = jnp.arange(B, dtype=jnp.int32)

    def one_pair(accum_total, inputs):
        blocks, obs_pair, mask_row = inputs
        rows_a = members[blocks[0] * B + offsets].astype(jnp.int32)
        rows_b = members[blocks[1] * B + offsets].astype(jnp.int32)
        spec_a = jnp.take(spectra, rows_a, axis=1).astype(jnp.float32)
        spec_b = jnp.take(spectra, rows_b, axis=1).astype(jnp.float32)
        a_real, a_imag = split_tiles(spec_a)
        b_real, b_imag = split_tiles(spec_b)
        mask_f = mask_row.astype(jnp.float32)
        day_count = jnp.sum(mask_f)
        masked_real = a_real * mask_f[:, None, None, None]
        masked_imag = a_imag * mask_f[:, None, None, None]
        cross_real = jnp.einsum('dakj,dbkj->dabkj', masked_real, b_real) + jnp.einsum('dakj,dbkj->dabkj', masked_imag, b_imag)
        cross_imag = jnp.einsum('dakj,dbkj->dabkj', masked_imag, b_real) - jnp.einsum('dakj,dbkj->dabkj', masked_real, b_imag)
        cross = join_tiles(cross_real, cross_imag).astype(jnp.bfloat16)
        correlation = jnp.einsum('dabc,cl->abl', cross.astype(jnp.float32), forward.astype(jnp.float32))
        stacked = correlation / day_count
        residual = weighted_residual(stacked, obs_pair.astype(jnp.float32), hilbert)
        response = jnp.dot(residual.reshape(B * B, L), backward_f, precision=lax.Precision.HIGHEST, preferred_element_type=jnp.float32)
        g_cos, g_sin = split_tiles(response.reshape(B, B, 2 * F))
        day_share = mask_f / day_count
        adj_a_real = jnp.einsum('abkj,dbkj->dakj', g_cos, b_real) + jnp.einsum('abkj,dbkj->dakj', g_sin, b_imag)
        adj_a_imag = jnp.einsum('abkj,dbkj->dakj', g_cos, b_imag) - jnp.einsum('abkj,dbkj->dakj', g_sin, b_real)
        adj_b_real = jnp.einsum('abkj,dakj->dbkj', g_cos, a_real) - jnp.einsum('abkj,dakj->dbkj', g_sin, a_imag)
        adj_b_imag = jnp.einsum('abkj,dakj->dbkj', g_cos, a_imag) + jnp.einsum('abkj,dakj->dbkj', g_sin, a_real)
        side_a = join_tiles(adj_a_real, adj_a_imag) * day_share[:, None, None]
        side_b = join_tiles(adj_b_real, adj_b_imag) * day_share[:, None, None]
        accum_total = accum_total.at[:, rows_a].add(side_a)
        accum_total = accum_total.at[:, rows_b].add(side_b)
        return (accum_total, None)
    start = jnp.zeros((DAYS, NSTA, 2 * F), jnp.float32)
    accum_total, _ = lax.scan(one_pair, start, (pair_blocks, observed, day_mask))
    return accum_total
```

```python
import functools

import jax
import jax.numpy as jnp
import numpy as np
from jax import lax
from jax.experimental import pallas as pl
from jax.experimental.pallas import tpu as pltpu
from jax.sharding import PartitionSpec as P

B = 64
F = 1024
L = 128
NBLK = 8
NSTA = 512
N1 = 16
N2 = 8
NQ = 16
NY = 4
NC = NQ * NY
ROWS = 96
MESH = pl.DeviceIdType.MESH
F32 = jnp.float32
BF16 = jnp.bfloat16


def phase_tables():
    freq = 64 * np.arange(NQ)[:, None] + np.arange(128)[None, :] % 64
    sign = np.where(np.arange(128) < 64, -1.0, 1.0)[None, None, :]
    shift_a = N2 * np.arange(N1) - L // 2
    shift_b = -np.arange(N2)
    tables = []
    for shift in (shift_a, shift_b):
        turns = (freq[:, None, :] * shift[None, :, None]) % (2 * F)
        angle = np.pi * turns / F
        tables.append(np.cos(angle).astype(np.float32))
        tables.append((np.sin(angle) * sign).astype(np.float32))
    return tables


def hilbert_blocks():
    blocks = []
    for k in (1, 3, 5, 7):
        offset = (8 * (np.arange(N1)[:, None] - np.arange(N1)[None, :]) + k) % L
        angle = np.pi * offset / L
        value = 2.0 / L * np.cos(angle) / np.sin(angle)
        blocks.append(np.kron(value, np.eye(16)))
    exact = np.stack(blocks).astype(np.float32)
    high = exact.astype(jnp.bfloat16)
    low = (exact - high.astype(np.float32)).astype(jnp.bfloat16)
    return high, low


def dot(a, b):
    return lax.dot_general(a, b, (((1,), (0,)), ((), ())), preferred_element_type=F32)


def kernel(
    mask_ref, idc_ref, ids_ref, spec_ref, obs_ref, ca_ref, sa_ref, cb_ref, sb_ref,
    kh_ref, kl_ref, out_ref,
    stage, xin, amod, bmod, acc, acc_in, envo, rfull, rturn, tbuf, ubuf, outb, rin,
    send_a, recv_a, send_d, recv_d, send_x, recv_x,
):
    q_me = lax.axis_index("pairs")
    d_me = lax.axis_index("days")
    y_me = d_me // 2
    k_me = lax.rem(d_me, 2)
    c_me = q_me * NY + y_me
    z_me = q_me // 4
    x_me = lax.rem(q_me, 4)
    pp = y_me // 2
    partner = (q_me, y_me * 2 + 1 - k_me)

    barrier = pltpu.get_barrier_semaphore()

    def greet(c, carry):
        @pl.when(c != c_me)
        def _():
            pl.semaphore_signal(
                barrier, inc=1, device_id=(c // NY, lax.rem(c, NY) * 2 + k_me), device_id_type=MESH
            )

        return carry

    lax.fori_loop(0, NC, greet, 0)
    pl.semaphore_signal(barrier, inc=1, device_id=partner, device_id_type=MESH)

    pl.semaphore_wait(barrier, NC)

    def target(step):
        q = lax.rem(z_me + step // 4, 4) * 4 + lax.rem(x_me + lax.rem(step, 4), 4)
        return q

    def source(step):
        q = lax.rem(z_me + 4 - step // 4, 4) * 4 + lax.rem(x_me + 4 - lax.rem(step, 4), 4)
        return q

    def copy_a(c, slot):
        return pltpu.make_async_remote_copy(
            src_ref=stage.at[c],
            dst_ref=xin.at[slot],
            send_sem=send_a.at[c],
            recv_sem=recv_a.at[slot],
            device_id=(c // NY, lax.rem(c, NY) * 2 + k_me),
            device_id_type=MESH,
        )

    def copy_d(c, slot):
        return pltpu.make_async_remote_copy(
            src_ref=outb.at[c],
            dst_ref=rin.at[slot],
            send_sem=send_d.at[c],
            recv_sem=recv_d.at[slot],
            device_id=(c // NY, lax.rem(c, NY) * 2 + k_me),
            device_id_type=MESH,
        )

    lane_q = lax.broadcasted_iota(jnp.int32, (NY * ROWS, NQ), 1)
    lane_s = lax.broadcasted_iota(jnp.int32, (NY * ROWS, NSTA), 1)

    def send_all(step, carry):
        q = target(step)
        row_id = jnp.sum(jnp.where(lane_q == q, idc_ref[...], 0), axis=1, keepdims=True)
        select = (lane_s == row_id).astype(F32).astype(BF16)
        rows = dot(select, spec_ref[...]).astype(BF16)
        stage[pl.ds(q * NY, NY)] = rows.reshape(NY, ROWS, 128)
        for i in range(NY):
            c = q * NY + lax.rem(y_me + i, NY)

            @pl.when(c != c_me)
            def _():
                copy_a(c, c_me).start()

        return carry

    lax.fori_loop(0, NQ, send_all, 0)
    xin[c_me] = stage[c_me]

    count = jnp.zeros((1, 128), F32)
    for d in range(8):
        count = count + mask_ref[pp, d].astype(F32)

    def hilbert(high, low):
        lane = lax.broadcasted_iota(jnp.int32, (256, 512), 1)
        total = None
        for j, k in enumerate((1, 3, 5, 7)):
            part = dot(kh_ref[j], high) + dot(kl_ref[j], high)
            if low is not None:
                part = part + dot(kh_ref[j], low)
            part = pltpu.roll(part, 64 * k, 1)
            part = jnp.where(lane < 64 * k, pltpu.roll(part, 16, 0), part)
            total = part if total is None else total + part
        return total

    obs_f = obs_ref[...].astype(F32)
    hil_o = hilbert(obs_ref[...], None)
    envo[...] = jnp.sqrt(obs_f * obs_f + hil_o * hil_o)

    acc[...] = jnp.zeros_like(acc)

    def forward(step, carry):
        q = source(step)
        for y in range(NY):
            c = q * NY + y

            @pl.when(c != c_me)
            def _():
                copy_a(c, c).wait_recv()

        for y in range(NY):
            keep = mask_ref[pp, 2 * y + k_me].astype(F32)
            x = xin[q * NY + y].astype(F32) * keep
            xr = pltpu.roll(x, 64, 1)
            lanes = slice(y * 128, (y + 1) * 128)
            for h in range(2):
                rows = slice(h * 16, (h + 1) * 16)
                for n in range(N1):
                    turned = x[rows] * ca_ref[q, n : n + 1, :] + xr[rows] * sa_ref[q, n : n + 1, :]
                    amod[q, h * 256 + n * 16 : h * 256 + (n + 1) * 16, lanes] = turned.astype(BF16)
            for n in range(N2):
                turned = x[32:] * cb_ref[q, n : n + 1, :] + xr[32:] * sb_ref[q, n : n + 1, :]
                bmod[q, n * 64 : (n + 1) * 64, lanes] = turned.astype(BF16)
        for h in range(2):
            acc[h] += lax.dot_general(
                amod[q, h * 256 : (h + 1) * 256, :],
                bmod[q],
                (((1,), (1,)), ((), ())),
                preferred_element_type=F32,
            )
        return carry

    lax.fori_loop(0, NQ, forward, 0)

    swap = pltpu.make_async_remote_copy(
        src_ref=acc.at[1 - k_me],
        dst_ref=acc_in,
        send_sem=send_x.at[0],
        recv_sem=recv_x.at[0],
        device_id=partner,
        device_id_type=MESH,
    )
    swap.start()
    swap.wait_recv()
    lanes_count = jnp.concatenate([count] * 4, axis=1)
    stacked = (acc[k_me] + acc_in[...]) * (1.0 / 32.0) / lanes_count
    high = stacked.astype(BF16)
    low = (stacked - high.astype(F32)).astype(BF16)
    hil_s = hilbert(high, low)
    env_s = jnp.sqrt(stacked * stacked + hil_s * hil_s)
    residual = (stacked - obs_ref[...].astype(F32)) * (
        (1.0 + env_s) / (1.0 + env_s + envo[...])
    )
    rfull[k_me] = (residual * (1.0 / 32.0) / lanes_count).astype(BF16)
    share = pltpu.make_async_remote_copy(
        src_ref=rfull.at[k_me],
        dst_ref=rfull.at[k_me],
        send_sem=send_x.at[1],
        recv_sem=recv_x.at[1],
        device_id=partner,
        device_id_type=MESH,
    )
    share.start()
    pltpu.make_async_remote_copy(
        src_ref=rfull.at[1 - k_me],
        dst_ref=rfull.at[1 - k_me],
        send_sem=send_x.at[1],
        recv_sem=recv_x.at[1],
        device_id=partner,
        device_id_type=MESH,
    ).wait_recv()
    rturn[...] = rfull[...].reshape(512, 512).T

    def adjoint(step, carry):
        q = target(step)
        for h in range(2):
            tbuf[h * 256 : (h + 1) * 256, :] = dot(rfull[h], bmod[q])
        for h in range(2):
            ubuf[h * 256 : (h + 1) * 256, :] = dot(rturn[h * 256 : (h + 1) * 256, :], amod[q])
        for y in range(NY):
            c = q * NY + y
            lanes = slice(y * 128, (y + 1) * 128)
            for h in range(2):
                straight = jnp.zeros((16, 128), F32)
                crossed = jnp.zeros((16, 128), F32)
                for n in range(N1):
                    t = tbuf[h * 256 + n * 16 : h * 256 + (n + 1) * 16, lanes]
                    straight = straight + t * ca_ref[q, n : n + 1, :]
                    crossed = crossed + t * sa_ref[q, n : n + 1, :]
                outb[c, h * 16 : (h + 1) * 16, :] = (
                    straight + pltpu.roll(crossed, 64, 1)
                ).astype(BF16)
            straight = jnp.zeros((64, 128), F32)
            crossed = jnp.zeros((64, 128), F32)
            for n in range(N2):
                u = ubuf[n * 64 : (n + 1) * 64, lanes]
                straight = straight + u * cb_ref[q, n : n + 1, :]
                crossed = crossed + u * sb_ref[q, n : n + 1, :]
            outb[c, 32:96, :] = (straight + pltpu.roll(crossed, 64, 1)).astype(BF16)
        for y in range(NY):
            c = q * NY + y

            @pl.when(c != c_me)
            def _():
                copy_d(c, c_me).start()

            @pl.when(c == c_me)
            def _():
                rin[c_me] = outb[c_me]

        return carry

    lax.fori_loop(0, NQ, adjoint, 0)

    out_ref[...] = jnp.zeros_like(out_ref)
    station = lax.broadcasted_iota(jnp.int32, (NSTA, NY * ROWS), 0)

    def gather(step, carry):
        q = source(step)
        for y in range(NY):
            c = q * NY + y

            @pl.when(c != c_me)
            def _():
                copy_d(c, c).wait_recv()

        place = (station == ids_ref[q]).astype(F32).astype(BF16)
        out_ref[...] += dot(place, rin[pl.ds(q * NY, NY)].reshape(NY * ROWS, 128))
        return carry

    lax.fori_loop(0, NQ, gather, 0)

    def drain(c, carry):
        @pl.when(c != c_me)
        def _():
            copy_a(c, c_me).wait_send()
            copy_d(c, c_me).wait_send()

        return carry

    lax.fori_loop(0, NC, drain, 0)
    swap.wait_send()
    share.wait_send()


def body(spectra, observed, pair_blocks, members, day_mask):
    y_me = lax.axis_index("days") // 2
    k_me = lax.rem(lax.axis_index("days"), 2)
    blocks = members.reshape(NBLK, B).astype(F32)
    pick = (pair_blocks[:, :, None] == jnp.arange(NBLK)[None, None, :]).astype(F32)
    ids = jnp.einsum("psn,nr->psr", pick, blocks, precision=lax.Precision.HIGHEST)
    ids = ids.astype(jnp.int32)
    ids_a = ids[:, 0].reshape(NQ, NY, 32)
    ids_b = jnp.broadcast_to(ids[:, 1].reshape(NQ, 2, 1, B), (NQ, 2, 2, B)).reshape(NQ, NY, B)
    ids_all = jnp.concatenate([ids_a, ids_b], axis=2).reshape(NQ, NY * ROWS)
    obs = lax.dynamic_slice(
        observed,
        (y_me // 2, lax.rem(y_me, 2) * 32 + k_me * 16, 0, 0),
        (1, 16, B, L),
    )
    obs = obs.reshape(16, B, N1, N2).transpose(2, 0, 3, 1).reshape(256, 512)
    ca, sa, cb, sb = phase_tables()
    kh, kl = hilbert_blocks()
    vm = pl.BlockSpec(memory_space=pltpu.VMEM)
    sm = pl.BlockSpec(memory_space=pltpu.SMEM)
    return pl.pallas_call(
        kernel,
        out_shape=jax.ShapeDtypeStruct((NSTA, 128), F32),
        in_specs=[sm] + [vm] * 10,
        out_specs=vm,
        scratch_shapes=[
            pltpu.VMEM((NC, ROWS, 128), BF16),
            pltpu.VMEM((NC, ROWS, 128), BF16),
            pltpu.VMEM((NQ, 512, 512), BF16),
            pltpu.VMEM((NQ, 512, 512), BF16),
            pltpu.VMEM((2, 256, 512), F32),
            pltpu.VMEM((256, 512), F32),
            pltpu.VMEM((256, 512), F32),
            pltpu.VMEM((2, 256, 512), BF16),
            pltpu.VMEM((512, 512), BF16),
            pltpu.VMEM((512, 512), F32),
            pltpu.VMEM((512, 512), F32),
            pltpu.VMEM((NC, ROWS, 128), BF16),
            pltpu.VMEM((NC, ROWS, 128), BF16),
            pltpu.SemaphoreType.DMA((NC,)),
            pltpu.SemaphoreType.DMA((NC,)),
            pltpu.SemaphoreType.DMA((NC,)),
            pltpu.SemaphoreType.DMA((NC,)),
            pltpu.SemaphoreType.DMA((2,)),
            pltpu.SemaphoreType.DMA((2,)),
        ],
        compiler_params=pltpu.CompilerParams(
            collective_id=0, has_side_effects=True, vmem_limit_bytes=60 * 1024 * 1024
        ),
        name="stack_adjoint",
    )(
        day_mask,
        ids_all.T,
        ids_all.reshape(NQ, 1, NY * ROWS),
        spectra[0],
        obs,
        ca,
        sa,
        cb,
        sb,
        kh,
        kl,
    )[None]


def solution(mesh):
    return jax.shard_map(
        body,
        mesh=mesh,
        in_specs=(
            P("days", None, "pairs"),
            P("pairs", None, None, None),
            P(),
            P(),
            P("pairs", None),
        ),
        out_specs=P("days", None, "pairs"),
        check_vma=False,
    )
```

```python
import functools

import jax
import jax.numpy as jnp
import numpy as np
from jax import lax
from jax.experimental import pallas as pl
from jax.experimental.pallas import tpu as pltpu
from jax.sharding import PartitionSpec as P

B = 64
F = 1024
L = 128
NBLK = 8
NSTA = 512
N1 = 16
N2 = 8
NQ = 16
NY = 4
NC = NQ * NY
ROWS = 96
MESH = pl.DeviceIdType.MESH
F32 = jnp.float32
BF16 = jnp.bfloat16


def phase_tables():
    freq = 64 * np.arange(NQ)[:, None] + np.arange(128)[None, :] % 64
    sign = np.where(np.arange(128) < 64, -1.0, 1.0)[None, None, :]
    tables = []
    for shift in (N2 * np.arange(N1) - L // 2, -np.arange(N2)):
        turns = (freq[:, None, :] * shift[None, :, None]) % (2 * F)
        angle = np.pi * turns / F
        tables += [np.cos(angle), np.sin(angle) * sign]
    return np.concatenate(tables, axis=1).astype(np.float32)


CA, SA, CB, SB = 0, N1, 2 * N1, 2 * N1 + N2


def hilbert_band():
    blocks = []
    for k in range(7, -7, -2):
        offset = (8 * (np.arange(N1)[:, None] - np.arange(N1)[None, :]) + k) % L
        angle = np.pi * offset / L
        value = 2.0 / L * np.cos(angle) / np.sin(angle)
        blocks.append(np.kron(value, np.eye(16)))
    return np.concatenate(blocks, axis=1).astype(np.float32).astype(jnp.bfloat16)


def dot(a, b):
    return lax.dot_general(a, b, (((1,), (0,)), ((), ())), preferred_element_type=F32)


def kernel(
    mask_ref, ids_ref, spec_ref, obs_hbm, tab_hbm, band_hbm, out_ref,
    stage, xin, amod, bmod, acc, acc_in, obsr, obst, obsf, envo, xst, idc, tab, band,
    rfull, rturn, tbuf, ubuf, outb, rin,
    send_a, recv_a, send_d, recv_d, send_x, recv_x, load,
):
    q_me = lax.axis_index("pairs")
    d_me = lax.axis_index("days")
    y_me = d_me // 2
    k_me = lax.rem(d_me, 2)
    c_me = q_me * NY + y_me
    z_me = q_me // 4
    x_me = lax.rem(q_me, 4)
    pp = y_me // 2
    partner = (q_me, y_me * 2 + 1 - k_me)

    barrier = pltpu.get_barrier_semaphore()

    row_a = lax.rem(y_me, 2) * 32 + k_me * 16
    loads = [
        pltpu.make_async_copy(obs_hbm.at[pp, pl.ds(row_a, 16)], obsr, load.at[0]),
        pltpu.make_async_copy(band_hbm, band, load.at[1]),
        pltpu.make_async_copy(tab_hbm, tab, load.at[2]),
    ]
    for copy in loads:
        copy.start()

    def greet(c, carry):
        @pl.when(c != c_me)
        def _():
            pl.semaphore_signal(
                barrier, inc=1, device_id=(c // NY, lax.rem(c, NY) * 2 + k_me), device_id_type=MESH
            )

        return carry

    lax.fori_loop(0, NC, greet, 0)
    pl.semaphore_signal(barrier, inc=1, device_id=partner, device_id_type=MESH)

    idc[...] = ids_ref[...].astype(F32).T
    lane_q = lax.broadcasted_iota(jnp.int32, (NY * ROWS, NQ), 1)
    lane_s = lax.broadcasted_iota(jnp.int32, (NY * ROWS, NSTA), 1).astype(F32)

    def fill(q, carry):
        row_id = jnp.sum(jnp.where(lane_q == q, idc[...], 0.0), axis=1, keepdims=True)
        select = (lane_s == row_id).astype(F32).astype(BF16)
        rows = dot(select, spec_ref[...]).astype(BF16)
        stage[pl.ds(q * NY, NY)] = rows.reshape(NY, ROWS, 128)
        return carry

    lax.fori_loop(0, NQ, fill, 0)
    pl.semaphore_wait(barrier, NC)

    def offsets(step):
        dx = lax.rem(17 - step, 4)
        dz = lax.rem((15 - step) // 4 + 2 + dx, 4)
        return dx, dz

    def target(step):
        dx, dz = offsets(step)
        return lax.rem(z_me + dz, 4) * 4 + lax.rem(x_me + dx, 4)

    def source(step):
        dx, dz = offsets(step)
        return lax.rem(z_me + 4 - dz, 4) * 4 + lax.rem(x_me + 4 - dx, 4)

    def copy_a(c, slot):
        return pltpu.make_async_remote_copy(
            src_ref=stage.at[c],
            dst_ref=xin.at[slot],
            send_sem=send_a.at[c],
            recv_sem=recv_a.at[slot],
            device_id=(c // NY, lax.rem(c, NY) * 2 + k_me),
            device_id_type=MESH,
        )

    def copy_d(c, slot):
        return pltpu.make_async_remote_copy(
            src_ref=outb.at[c],
            dst_ref=rin.at[slot],
            send_sem=send_d.at[c],
            recv_sem=recv_d.at[slot],
            device_id=(c // NY, lax.rem(c, NY) * 2 + k_me),
            device_id_type=MESH,
        )

    def send_all(step, carry):
        q = target(step)
        for dy in (2, 1, 3, 0):
            c = q * NY + lax.rem(y_me + dy, NY)

            @pl.when(c != c_me)
            def _():
                copy_a(c, c_me).start()

        return carry

    lax.fori_loop(0, NQ, send_all, 0)
    xin[c_me] = stage[c_me]

    count = jnp.zeros((1, 128), F32)
    for d in range(8):
        count = count + mask_ref[pp, d].astype(F32)

    lane = lax.broadcasted_iota(jnp.int32, (1, 128), 1)

    def hilbert(value):
        for j in range(4):
            swapped = pltpu.roll(value[:, j * 128 : (j + 1) * 128], 64, 1)
            xst[j * 256 : (j + 1) * 256, :] = swapped.astype(BF16)
        part = [dot(band[:, (3 - t) * 256 : (7 - t) * 256], xst[...]) for t in range(4)]
        wrapped = [pltpu.roll(part[3], 16, 0)] + part
        return jnp.concatenate(
            [jnp.where(lane < 64, wrapped[j], wrapped[j + 1]) for j in range(4)], axis=1
        )

    loads[0].wait()

    def turn(a, carry):
        one = obsr[a].astype(F32)
        obst[pl.ds(pl.multiple_of(a * 128, 128), 128), :] = jnp.concatenate([one, one], axis=0).T
        return carry

    lax.fori_loop(0, 16, turn, 0)

    def place_lags(n, carry):
        for j in range(4):
            first = obst[pl.ds(n * 8 + 2 * j, 16, stride=128), :]
            second = obst[pl.ds(n * 8 + 2 * j + 1, 16, stride=128), :]
            obsf[pl.ds(pl.multiple_of(n * 16, 16), 16), j * 128 : (j + 1) * 128] = jnp.where(
                lane < 64, first, second
            )
        return carry

    lax.fori_loop(0, N1, place_lags, 0)
    loads[1].wait()
    obs_f = obsf[...]
    hil_o = hilbert(obs_f)
    envo[...] = jnp.sqrt(obs_f * obs_f + hil_o * hil_o)

    acc[...] = jnp.zeros_like(acc)
    loads[2].wait()

    def forward(step, carry):
        q = source(step)
        for y in range(NY):
            c = q * NY + y

            @pl.when(c != c_me)
            def _():
                copy_a(c, c).wait_recv()

        for y in range(NY):
            keep = mask_ref[pp, 2 * y + k_me].astype(F32)
            x = xin[q * NY + y].astype(F32) * keep
            xr = pltpu.roll(x, 64, 1)
            lanes = slice(y * 128, (y + 1) * 128)
            for h in range(2):
                rows = slice(h * 16, (h + 1) * 16)
                for n in range(N1):
                    turned = x[rows] * tab[q, CA + n : CA + n + 1, :] + xr[rows] * tab[q, SA + n : SA + n + 1, :]
                    amod[q, h * 256 + n * 16 : h * 256 + (n + 1) * 16, lanes] = turned.astype(BF16)
            for n in range(N2):
                turned = x[32:] * tab[q, CB + n : CB + n + 1, :] + xr[32:] * tab[q, SB + n : SB + n + 1, :]
                bmod[q, n * 64 : (n + 1) * 64, lanes] = turned.astype(BF16)
        for h in range(2):
            acc[h] += lax.dot_general(
                amod[q, h * 256 : (h + 1) * 256, :],
                bmod[q],
                (((1,), (1,)), ((), ())),
                preferred_element_type=F32,
            )
        return carry

    lax.fori_loop(0, NQ, forward, 0)

    swap = pltpu.make_async_remote_copy(
        src_ref=acc.at[1 - k_me],
        dst_ref=acc_in,
        send_sem=send_x.at[0],
        recv_sem=recv_x.at[0],
        device_id=partner,
        device_id_type=MESH,
    )
    swap.start()
    swap.wait_recv()
    lanes_count = jnp.concatenate([count] * 4, axis=1)
    stacked = (acc[k_me] + acc_in[...]) * (1.0 / 32.0) / lanes_count
    hil_s = hilbert(stacked)
    env_s = jnp.sqrt(stacked * stacked + hil_s * hil_s)
    residual = (stacked - obsf[...]) * (
        (1.0 + env_s) / (1.0 + env_s + envo[...])
    )
    rfull[k_me] = (residual * (1.0 / 32.0) / lanes_count).astype(BF16)
    share = pltpu.make_async_remote_copy(
        src_ref=rfull.at[k_me],
        dst_ref=rfull.at[k_me],
        send_sem=send_x.at[1],
        recv_sem=recv_x.at[1],
        device_id=partner,
        device_id_type=MESH,
    )
    share.start()
    pltpu.make_async_remote_copy(
        src_ref=rfull.at[1 - k_me],
        dst_ref=rfull.at[1 - k_me],
        send_sem=send_x.at[1],
        recv_sem=recv_x.at[1],
        device_id=partner,
        device_id_type=MESH,
    ).wait_recv()
    rturn[...] = rfull[...].reshape(512, 512).T

    def adjoint(step, carry):
        q = target(step)
        for h in range(2):
            tbuf[h * 256 : (h + 1) * 256, :] = dot(rfull[h], bmod[q])
        for h in range(2):
            ubuf[h * 256 : (h + 1) * 256, :] = dot(rturn[h * 256 : (h + 1) * 256, :], amod[q])
        for y in range(NY):
            c = q * NY + y
            lanes = slice(y * 128, (y + 1) * 128)
            for h in range(2):
                straight = jnp.zeros((16, 128), F32)
                crossed = jnp.zeros((16, 128), F32)
                for n in range(N1):
                    t = tbuf[h * 256 + n * 16 : h * 256 + (n + 1) * 16, lanes]
                    straight = straight + t * tab[q, CA + n : CA + n + 1, :]
                    crossed = crossed + t * tab[q, SA + n : SA + n + 1, :]
                outb[c, h * 16 : (h + 1) * 16, :] = (
                    straight + pltpu.roll(crossed, 64, 1)
                ).astype(BF16)
            straight = jnp.zeros((64, 128), F32)
            crossed = jnp.zeros((64, 128), F32)
            for n in range(N2):
                u = ubuf[n * 64 : (n + 1) * 64, lanes]
                straight = straight + u * tab[q, CB + n : CB + n + 1, :]
                crossed = crossed + u * tab[q, SB + n : SB + n + 1, :]
            outb[c, 32:96, :] = (straight + pltpu.roll(crossed, 64, 1)).astype(BF16)
        for y in range(NY):
            c = q * NY + y

            @pl.when(c != c_me)
            def _():
                copy_d(c, c_me).start()

            @pl.when(c == c_me)
            def _():
                rin[c_me] = outb[c_me]

        return carry

    lax.fori_loop(0, NQ, adjoint, 0)

    out_ref[...] = jnp.zeros_like(out_ref)
    station = lax.broadcasted_iota(jnp.int32, (NSTA, NY * ROWS), 0)

    def gather(step, carry):
        q = source(step)
        for y in range(NY):
            c = q * NY + y

            @pl.when(c != c_me)
            def _():
                copy_d(c, c).wait_recv()

        place = (station == ids_ref[pl.ds(q, 1), :]).astype(F32).astype(BF16)
        out_ref[...] += dot(place, rin[pl.ds(q * NY, NY)].reshape(NY * ROWS, 128))
        return carry

    lax.fori_loop(0, NQ, gather, 0)

    def drain(c, carry):
        @pl.when(c != c_me)
        def _():
            copy_a(c, c_me).wait_send()
            copy_d(c, c_me).wait_send()

        return carry

    lax.fori_loop(0, NC, drain, 0)
    swap.wait_send()
    share.wait_send()


def body(spectra, observed, pair_blocks, members, day_mask):
    blocks = members.reshape(NBLK, B).astype(F32)
    pick = (pair_blocks[:, :, None] == jnp.arange(NBLK)[None, None, :]).astype(F32)
    ids = jnp.einsum("psn,nr->psr", pick, blocks, precision=lax.Precision.HIGHEST)
    ids = ids.astype(jnp.int32)
    ids_a = ids[:, 0].reshape(NQ, NY, 32)
    ids_b = jnp.broadcast_to(ids[:, 1].reshape(NQ, 2, 1, B), (NQ, 2, 2, B)).reshape(NQ, NY, B)
    ids_all = jnp.concatenate([ids_a, ids_b], axis=2).reshape(NQ, NY * ROWS)
    vm = pl.BlockSpec(memory_space=pltpu.VMEM)
    sm = pl.BlockSpec(memory_space=pltpu.SMEM)
    hbm = pl.BlockSpec(memory_space=pltpu.HBM)
    return pl.pallas_call(
        kernel,
        out_shape=jax.ShapeDtypeStruct((NSTA, 128), F32),
        in_specs=[sm, vm, vm, hbm, hbm, hbm],
        out_specs=vm,
        scratch_shapes=[
            pltpu.VMEM((NC, ROWS, 128), BF16),
            pltpu.VMEM((NC, ROWS, 128), BF16),
            pltpu.VMEM((NQ, 512, 512), BF16),
            pltpu.VMEM((NQ, 512, 512), BF16),
            pltpu.VMEM((2, 256, 512), F32),
            pltpu.VMEM((256, 512), F32),
            pltpu.VMEM((16, B, L), BF16),
            pltpu.VMEM((16 * L, 128), F32),
            pltpu.VMEM((256, 512), F32),
            pltpu.VMEM((256, 512), F32),
            pltpu.VMEM((4 * 256, 128), BF16),
            pltpu.VMEM((NY * ROWS, NQ), F32),
            pltpu.VMEM((NQ, 2 * (N1 + N2), 128), F32),
            pltpu.VMEM((256, 7 * 256), BF16),
            pltpu.VMEM((2, 256, 512), BF16),
            pltpu.VMEM((512, 512), BF16),
            pltpu.VMEM((512, 512), F32),
            pltpu.VMEM((512, 512), F32),
            pltpu.VMEM((NC, ROWS, 128), BF16),
            pltpu.VMEM((NC, ROWS, 128), BF16),
            pltpu.SemaphoreType.DMA((NC,)),
            pltpu.SemaphoreType.DMA((NC,)),
            pltpu.SemaphoreType.DMA((NC,)),
            pltpu.SemaphoreType.DMA((NC,)),
            pltpu.SemaphoreType.DMA((2,)),
            pltpu.SemaphoreType.DMA((2,)),
            pltpu.SemaphoreType.DMA((3,)),
        ],
        compiler_params=pltpu.CompilerParams(
            collective_id=0, has_side_effects=True, vmem_limit_bytes=56000000
        ),
        name="stack_adjoint",
    )(
        day_mask,
        ids_all,
        spectra[0],
        observed,
        phase_tables(),
        hilbert_band(),
    )[None]


def solution(mesh):
    return jax.shard_map(
        body,
        mesh=mesh,
        in_specs=(
            P("days", None, "pairs"),
            P("pairs", None, None, None),
            P(),
            P(),
            P("pairs", None),
        ),
        out_specs=P("days", None, "pairs"),
        check_vma=False,
    )
```

```python
import functools

import jax
import jax.numpy as jnp
import numpy as np
from jax import lax
from jax.experimental import pallas as pl
from jax.experimental.pallas import tpu as pltpu
from jax.sharding import PartitionSpec as P

B = 64
F = 1024
L = 128
NBLK = 8
NSTA = 512
N1 = 16
N2 = 8
NQ = 16
NY = 4
NC = NQ * NY
ROWS = 96
MESH = pl.DeviceIdType.MESH
F32 = jnp.float32
BF16 = jnp.bfloat16


def phase_tables():
    freq = 64 * np.arange(NQ)[:, None] + np.arange(128)[None, :] % 64
    sign = np.where(np.arange(128) < 64, -1.0, 1.0)[None, None, :]
    tables = []
    for shift in (N2 * np.arange(N1) - L // 2, -np.arange(N2)):
        turns = (freq[:, None, :] * shift[None, :, None]) % (2 * F)
        angle = np.pi * turns / F
        tables += [np.cos(angle), np.sin(angle) * sign]
    return np.concatenate(tables, axis=1).astype(np.float32)


CA, SA, CB, SB = 0, N1, 2 * N1, 2 * N1 + N2


def hilbert_band():
    blocks = []
    for k in range(7, -7, -2):
        offset = (8 * (np.arange(N1)[:, None] - np.arange(N1)[None, :]) + k) % L
        angle = np.pi * offset / L
        value = 2.0 / L * np.cos(angle) / np.sin(angle)
        blocks.append(np.kron(value, np.eye(16)))
    return np.concatenate(blocks, axis=1).astype(np.float32).astype(jnp.bfloat16)


def dot(a, b):
    return lax.dot_general(a, b, (((1,), (0,)), ((), ())), preferred_element_type=F32)


def kernel(
    mask_hbm, pb_hbm, memb_hbm, spec_hbm, obs_hbm, tab_hbm, band_hbm, out_ref,
    mask_ref, pb, memb, spec, sperm, side, ids,
    stage, xin, amod, bmod, acc, acc_in, obsr, obst, obsf, envo, xst, tab, band,
    rfull, rturn, tbuf, ubuf, outb, rin,
    send_a, recv_a, send_d, recv_d, send_x, recv_x, load,
):
    q_me = lax.axis_index("pairs")
    d_me = lax.axis_index("days")
    y_me = d_me // 2
    k_me = lax.rem(d_me, 2)
    c_me = q_me * NY + y_me
    z_me = q_me // 4
    x_me = lax.rem(q_me, 4)
    pp = y_me // 2
    partner = (q_me, y_me * 2 + 1 - k_me)

    barrier = pltpu.get_barrier_semaphore()

    row_a = lax.rem(y_me, 2) * 32 + k_me * 16
    loads = [
        pltpu.make_async_copy(memb_hbm, memb, load.at[0]),
        pltpu.make_async_copy(pb_hbm, pb, load.at[1]),
        pltpu.make_async_copy(spec_hbm.at[0], spec, load.at[2]),
        pltpu.make_async_copy(mask_hbm, mask_ref, load.at[3]),
        pltpu.make_async_copy(obs_hbm.at[pp, pl.ds(row_a, 16)], obsr, load.at[4]),
        pltpu.make_async_copy(band_hbm, band, load.at[5]),
        pltpu.make_async_copy(tab_hbm, tab, load.at[6]),
    ]
    for copy in loads:
        copy.start()

    def greet(c, carry):
        @pl.when(c != c_me)
        def _():
            pl.semaphore_signal(
                barrier, inc=1, device_id=(c // NY, lax.rem(c, NY) * 2 + k_me), device_id_type=MESH
            )

        return carry

    lax.fori_loop(0, NC, greet, 0)
    pl.semaphore_signal(barrier, inc=1, device_id=partner, device_id_type=MESH)

    lane = lax.broadcasted_iota(jnp.int32, (1, 128), 1)
    loads[0].wait()
    column = jnp.concatenate([memb[...], memb[...]], axis=0).astype(F32).T
    loads[1].wait()
    pair_col = jnp.concatenate([pb[...]] * 4, axis=0).astype(F32).T
    loads[2].wait()
    lane_s = lax.broadcasted_iota(jnp.int32, (128, NSTA), 1).astype(F32)
    for j in range(4):
        select = (lane_s == column[:, j : j + 1]).astype(F32).astype(BF16)
        sperm[j * 128 : (j + 1) * 128, :] = dot(select, spec[...])

    side[0] = jnp.broadcast_to(pair_col[:, 0:1], (32, 128))
    side[1] = jnp.broadcast_to(pair_col[:, 1:2], (32, 128))
    both = jnp.where(lane < 64, side[0], side[1])
    names = jnp.zeros((32, 128), F32)
    for n in range(NBLK):
        row = memb[n // 2 : n // 2 + 1, :].astype(F32)
        other = pltpu.roll(row, 64, 1)
        row = jnp.where(lane < 64, row, other) if n % 2 == 0 else jnp.where(lane < 64, other, row)
        names = jnp.where(both == n, row, names)
    ids[...] = names

    def fill(pair, carry):
        rows = []
        for t in range(2):
            block = side[t, pl.ds(pair, 1), :]
            picked = sperm[0:64, :]
            for n in range(1, NBLK):
                picked = jnp.where(block == n, sperm[n * 64 : (n + 1) * 64, :], picked)
            rows.append(picked.astype(BF16))
        for h in range(2):
            stage[2 * pair + h, 0:32, :] = rows[0][h * 32 : (h + 1) * 32]
            stage[2 * pair + h, 32:96, :] = rows[1]
        return carry

    lax.fori_loop(0, 32, fill, 0)
    pl.semaphore_wait(barrier, NC)

    def offsets(step):
        dx = lax.rem(17 - step, 4)
        dz = lax.rem((15 - step) // 4 + 2 + dx, 4)
        return dx, dz

    def target(step):
        dx, dz = offsets(step)
        return lax.rem(z_me + dz, 4) * 4 + lax.rem(x_me + dx, 4)

    def source(step):
        dx, dz = offsets(step)
        return lax.rem(z_me + 4 - dz, 4) * 4 + lax.rem(x_me + 4 - dx, 4)

    def copy_a(c, slot):
        return pltpu.make_async_remote_copy(
            src_ref=stage.at[c],
            dst_ref=xin.at[slot],
            send_sem=send_a.at[c],
            recv_sem=recv_a.at[slot],
            device_id=(c // NY, lax.rem(c, NY) * 2 + k_me),
            device_id_type=MESH,
        )

    def copy_d(c, slot):
        return pltpu.make_async_remote_copy(
            src_ref=outb.at[c],
            dst_ref=rin.at[slot],
            send_sem=send_d.at[c],
            recv_sem=recv_d.at[slot],
            device_id=(c // NY, lax.rem(c, NY) * 2 + k_me),
            device_id_type=MESH,
        )

    def send_all(step, carry):
        q = target(step)
        for dy in (2, 1, 3, 0):
            c = q * NY + lax.rem(y_me + dy, NY)

            @pl.when(c != c_me)
            def _():
                copy_a(c, c_me).start()

        return carry

    lax.fori_loop(0, NQ, send_all, 0)
    xin[c_me] = stage[c_me]

    loads[3].wait()
    count = jnp.zeros((1, 128), F32)
    for d in range(8):
        count = count + mask_ref[pp, d].astype(F32)

    def hilbert(value):
        for j in range(4):
            swapped = pltpu.roll(value[:, j * 128 : (j + 1) * 128], 64, 1)
            xst[j * 256 : (j + 1) * 256, :] = swapped.astype(BF16)
        part = [dot(band[:, (3 - t) * 256 : (7 - t) * 256], xst[...]) for t in range(4)]
        wrapped = [pltpu.roll(part[3], 16, 0)] + part
        return jnp.concatenate(
            [jnp.where(lane < 64, wrapped[j], wrapped[j + 1]) for j in range(4)], axis=1
        )

    loads[4].wait()

    def turn(a, carry):
        one = obsr[a].astype(F32)
        obst[pl.ds(pl.multiple_of(a * 128, 128), 128), :] = jnp.concatenate([one, one], axis=0).T
        return carry

    lax.fori_loop(0, 16, turn, 0)

    def place_lags(n, carry):
        for j in range(4):
            first = obst[pl.ds(n * 8 + 2 * j, 16, stride=128), :]
            second = obst[pl.ds(n * 8 + 2 * j + 1, 16, stride=128), :]
            obsf[pl.ds(pl.multiple_of(n * 16, 16), 16), j * 128 : (j + 1) * 128] = jnp.where(
                lane < 64, first, second
            )
        return carry

    lax.fori_loop(0, N1, place_lags, 0)
    loads[5].wait()
    obs_f = obsf[...]
    hil_o = hilbert(obs_f)
    envo[...] = jnp.sqrt(obs_f * obs_f + hil_o * hil_o)

    acc[...] = jnp.zeros_like(acc)
    loads[6].wait()

    def forward(step, carry):
        q = source(step)
        for y in range(NY):
            c = q * NY + y

            @pl.when(c != c_me)
            def _():
                copy_a(c, c).wait_recv()

        for y in range(NY):
            keep = mask_ref[pp, 2 * y + k_me].astype(F32)
            x = xin[q * NY + y].astype(F32) * keep
            xr = pltpu.roll(x, 64, 1)
            lanes = slice(y * 128, (y + 1) * 128)
            for h in range(2):
                rows = slice(h * 16, (h + 1) * 16)
                for n in range(N1):
                    turned = x[rows] * tab[q, CA + n : CA + n + 1, :] + xr[rows] * tab[q, SA + n : SA + n + 1, :]
                    amod[q, h * 256 + n * 16 : h * 256 + (n + 1) * 16, lanes] = turned.astype(BF16)
            for n in range(N2):
                turned = x[32:] * tab[q, CB + n : CB + n + 1, :] + xr[32:] * tab[q, SB + n : SB + n + 1, :]
                bmod[q, n * 64 : (n + 1) * 64, lanes] = turned.astype(BF16)
        for h in range(2):
            acc[h] += lax.dot_general(
                amod[q, h * 256 : (h + 1) * 256, :],
                bmod[q],
                (((1,), (1,)), ((), ())),
                preferred_element_type=F32,
            )
        return carry

    lax.fori_loop(0, NQ, forward, 0)

    swap = pltpu.make_async_remote_copy(
        src_ref=acc.at[1 - k_me],
        dst_ref=acc_in,
        send_sem=send_x.at[0],
        recv_sem=recv_x.at[0],
        device_id=partner,
        device_id_type=MESH,
    )
    swap.start()
    swap.wait_recv()
    lanes_count = jnp.concatenate([count] * 4, axis=1)
    stacked = (acc[k_me] + acc_in[...]) * (1.0 / 32.0) / lanes_count
    hil_s = hilbert(stacked)
    env_s = jnp.sqrt(stacked * stacked + hil_s * hil_s)
    residual = (stacked - obsf[...]) * (
        (1.0 + env_s) / (1.0 + env_s + envo[...])
    )
    rfull[k_me] = (residual * (1.0 / 32.0) / lanes_count).astype(BF16)
    share = pltpu.make_async_remote_copy(
        src_ref=rfull.at[k_me],
        dst_ref=rfull.at[k_me],
        send_sem=send_x.at[1],
        recv_sem=recv_x.at[1],
        device_id=partner,
        device_id_type=MESH,
    )
    share.start()
    pltpu.make_async_remote_copy(
        src_ref=rfull.at[1 - k_me],
        dst_ref=rfull.at[1 - k_me],
        send_sem=send_x.at[1],
        recv_sem=recv_x.at[1],
        device_id=partner,
        device_id_type=MESH,
    ).wait_recv()
    rturn[...] = rfull[...].reshape(512, 512).T

    def adjoint(step, carry):
        q = target(step)
        for h in range(2):
            tbuf[h * 256 : (h + 1) * 256, :] = dot(rfull[h], bmod[q])
        for h in range(2):
            ubuf[h * 256 : (h + 1) * 256, :] = dot(rturn[h * 256 : (h + 1) * 256, :], amod[q])
        for y in range(NY):
            c = q * NY + y
            lanes = slice(y * 128, (y + 1) * 128)
            for h in range(2):
                straight = jnp.zeros((16, 128), F32)
                crossed = jnp.zeros((16, 128), F32)
                for n in range(N1):
                    t = tbuf[h * 256 + n * 16 : h * 256 + (n + 1) * 16, lanes]
                    straight = straight + t * tab[q, CA + n : CA + n + 1, :]
                    crossed = crossed + t * tab[q, SA + n : SA + n + 1, :]
                outb[c, h * 16 : (h + 1) * 16, :] = (
                    straight + pltpu.roll(crossed, 64, 1)
                ).astype(BF16)
            straight = jnp.zeros((64, 128), F32)
            crossed = jnp.zeros((64, 128), F32)
            for n in range(N2):
                u = ubuf[n * 64 : (n + 1) * 64, lanes]
                straight = straight + u * tab[q, CB + n : CB + n + 1, :]
                crossed = crossed + u * tab[q, SB + n : SB + n + 1, :]
            outb[c, 32:96, :] = (straight + pltpu.roll(crossed, 64, 1)).astype(BF16)

            @pl.when(c != c_me)
            def _():
                copy_d(c, c_me).start()

            @pl.when(c == c_me)
            def _():
                rin[c_me] = outb[c_me]

        return carry

    lax.fori_loop(0, NQ, adjoint, 0)

    out_ref[...] = jnp.zeros_like(out_ref)
    station = lax.broadcasted_iota(jnp.int32, (NSTA, 128), 0).astype(F32)
    blank = jnp.zeros((64, 128), BF16)

    def gather(step, carry):
        q = source(step)
        for y in range(NY):
            c = q * NY + y

            @pl.when(c != c_me)
            def _():
                copy_d(c, c).wait_recv()

        for half in range(2):
            c = q * NY + 2 * half
            place = (station == ids[pl.ds(2 * q + half, 1), :]).astype(F32).astype(BF16)
            rows = jnp.concatenate(
                [rin[c, 0:32, :], rin[c + 1, 0:32, :], rin[c, 32:96, :], blank, rin[c + 1, 32:96, :]],
                axis=0,
            )
            out_ref[...] += dot(jnp.concatenate([place, place], axis=1), rows)
        return carry

    lax.fori_loop(0, NQ, gather, 0)

    def drain(c, carry):
        @pl.when(c != c_me)
        def _():
            copy_a(c, c_me).wait_send()
            copy_d(c, c_me).wait_send()

        return carry

    lax.fori_loop(0, NC, drain, 0)
    swap.wait_send()
    share.wait_send()


def body(spectra, observed, pair_blocks, members, day_mask):
    vm = pl.BlockSpec(memory_space=pltpu.VMEM)
    hbm = pl.BlockSpec(memory_space=pltpu.HBM)
    return pl.pallas_call(
        kernel,
        out_shape=jax.ShapeDtypeStruct((NSTA, 128), F32),
        in_specs=[hbm] * 7,
        out_specs=vm,
        scratch_shapes=[
            pltpu.SMEM((2, 8), jnp.int32),
            pltpu.VMEM((2, 32), jnp.int32),
            pltpu.VMEM((4, 128), jnp.int32),
            pltpu.VMEM((NSTA, 128), BF16),
            pltpu.VMEM((NSTA, 128), F32),
            pltpu.VMEM((2, 32, 128), F32),
            pltpu.VMEM((32, 128), F32),
            pltpu.VMEM((NC, ROWS, 128), BF16),
            pltpu.VMEM((NC, ROWS, 128), BF16),
            pltpu.VMEM((NQ, 512, 512), BF16),
            pltpu.VMEM((NQ, 512, 512), BF16),
            pltpu.VMEM((2, 256, 512), F32),
            pltpu.VMEM((256, 512), F32),
            pltpu.VMEM((16, B, L), BF16),
            pltpu.VMEM((16 * L, 128), F32),
            pltpu.VMEM((256, 512), F32),
            pltpu.VMEM((256, 512), F32),
            pltpu.VMEM((4 * 256, 128), BF16),
            pltpu.VMEM((NQ, 2 * (N1 + N2), 128), F32),
            pltpu.VMEM((256, 7 * 256), BF16),
            pltpu.VMEM((2, 256, 512), BF16),
            pltpu.VMEM((512, 512), BF16),
            pltpu.VMEM((512, 512), F32),
            pltpu.VMEM((512, 512), F32),
            pltpu.VMEM((NC, ROWS, 128), BF16),
            pltpu.VMEM((NC, ROWS, 128), BF16),
            pltpu.SemaphoreType.DMA((NC,)),
            pltpu.SemaphoreType.DMA((NC,)),
            pltpu.SemaphoreType.DMA((NC,)),
            pltpu.SemaphoreType.DMA((NC,)),
            pltpu.SemaphoreType.DMA((2,)),
            pltpu.SemaphoreType.DMA((2,)),
            pltpu.SemaphoreType.DMA((7,)),
        ],
        compiler_params=pltpu.CompilerParams(
            collective_id=0, has_side_effects=True, vmem_limit_bytes=56000000
        ),
        name="stack_adjoint",
    )(
        *[
            pltpu.with_memory_space_constraint(value, pltpu.HBM)
            for value in (
                day_mask,
                pair_blocks.T,
                members.reshape(4, 128),
                spectra,
                observed,
                phase_tables(),
                hilbert_band(),
            )
        ],
    )[None]


def solution(mesh):
    return jax.shard_map(
        body,
        mesh=mesh,
        in_specs=(
            P("days", None, "pairs"),
            P("pairs", None, None, None),
            P(),
            P(),
            P("pairs", None),
        ),
        out_specs=P("days", None, "pairs"),
        check_vma=False,
    )
```

```python
import functools

import jax
import jax.numpy as jnp
import numpy as np
from jax import lax
from jax.experimental import pallas as pl
from jax.experimental.pallas import tpu as pltpu
from jax.sharding import PartitionSpec as P

B = 64
F = 1024
L = 128
NBLK = 8
NSTA = 512
N1 = 16
N2 = 8
NQ = 16
NY = 4
NC = NQ * NY
ROWS = 96
MESH = pl.DeviceIdType.MESH
F32 = jnp.float32
BF16 = jnp.bfloat16


def phase_tables():
    freq = 64 * np.arange(NQ)[:, None] + np.arange(128)[None, :] % 64
    sign = np.where(np.arange(128) < 64, -1.0, 1.0)[None, None, :]
    tables = []
    for shift in (N2 * np.arange(N1) - L // 2, -np.arange(N2)):
        turns = (freq[:, None, :] * shift[None, :, None]) % (2 * F)
        angle = np.pi * turns / F
        tables += [np.cos(angle), np.sin(angle) * sign]
    return np.concatenate(tables, axis=1).astype(np.float32)


CA, SA, CB, SB = 0, N1, 2 * N1, 2 * N1 + N2


def hilbert_band():
    blocks = []
    for k in range(7, -7, -2):
        offset = (8 * (np.arange(N1)[:, None] - np.arange(N1)[None, :]) + k) % L
        angle = np.pi * offset / L
        value = 2.0 / L * np.cos(angle) / np.sin(angle)
        blocks.append(np.kron(value, np.eye(16)))
    return np.concatenate(blocks, axis=1).astype(np.float32).astype(jnp.bfloat16)


def dot(a, b):
    return lax.dot_general(a, b, (((1,), (0,)), ((), ())), preferred_element_type=F32)


def kernel(
    mask_hbm, pb_hbm, memb_hbm, spec_hbm, obs_hbm, tab_hbm, band_hbm, out_ref,
    mask_ref, pb, memb, spec, sperm, side, ids,
    stage, xin, amod_e, amod_o, bmod_e, bmod_o, acc, acc_out, acc_in, obsr, obst, obsf, envo, xst, tab, band,
    rfull, rturn, tbuf_e, tbuf_o, ubuf_e, ubuf_o, outb, rin,
    send_a, recv_a, send_d, recv_d, send_x, recv_x, load,
):
    q_me = lax.axis_index("pairs")
    d_me = lax.axis_index("days")
    y_me = d_me // 2
    k_me = lax.rem(d_me, 2)
    c_me = q_me * NY + y_me
    z_me = q_me // 4
    x_me = lax.rem(q_me, 4)
    pp = y_me // 2
    partner = (q_me, y_me * 2 + 1 - k_me)

    barrier = pltpu.get_barrier_semaphore()

    row_a = lax.rem(y_me, 2) * 32 + k_me * 16
    loads = [
        pltpu.make_async_copy(memb_hbm, memb, load.at[0]),
        pltpu.make_async_copy(pb_hbm, pb, load.at[1]),
        pltpu.make_async_copy(spec_hbm.at[0], spec, load.at[2]),
        pltpu.make_async_copy(mask_hbm, mask_ref, load.at[3]),
        pltpu.make_async_copy(obs_hbm.at[pp, pl.ds(row_a, 16)], obsr, load.at[4]),
        pltpu.make_async_copy(band_hbm, band, load.at[5]),
        pltpu.make_async_copy(tab_hbm, tab, load.at[6]),
    ]
    for copy in loads:
        copy.start()

    def greet(c, carry):
        @pl.when(c != c_me)
        def _():
            pl.semaphore_signal(
                barrier, inc=1, device_id=(c // NY, lax.rem(c, NY) * 2 + k_me), device_id_type=MESH
            )

        return carry

    lax.fori_loop(0, NC, greet, 0)
    pl.semaphore_signal(barrier, inc=1, device_id=partner, device_id_type=MESH)

    lane = lax.broadcasted_iota(jnp.int32, (1, 128), 1)
    loads[0].wait()
    column = jnp.concatenate([memb[...], memb[...]], axis=0).astype(F32).T
    loads[1].wait()
    pair_col = jnp.concatenate([pb[...]] * 4, axis=0).astype(F32).T
    loads[2].wait()
    lane_s = lax.broadcasted_iota(jnp.int32, (128, NSTA), 1).astype(F32)
    for j in range(4):
        select = (lane_s == column[:, j : j + 1]).astype(F32).astype(BF16)
        sperm[j * 128 : (j + 1) * 128, :] = dot(select, spec[...])

    side[0] = jnp.broadcast_to(pair_col[:, 0:1], (32, 128))
    side[1] = jnp.broadcast_to(pair_col[:, 1:2], (32, 128))
    def fill(pair, carry):
        rows = []
        for t in range(2):
            block = side[t, pl.ds(pair, 1), :]
            picked = sperm[0:64, :]
            for n in range(1, NBLK):
                picked = jnp.where(block == n, sperm[n * 64 : (n + 1) * 64, :], picked)
            rows.append(picked.astype(BF16))
        for h in range(2):
            stage[2 * pair + h, 0:32, :] = rows[0][h * 32 : (h + 1) * 32]
            stage[2 * pair + h, 32:96, :] = rows[1]
        return carry

    lax.fori_loop(0, 32, fill, 0)
    pl.semaphore_wait(barrier, NC)

    def offsets(step):
        dx = lax.rem(17 - step, 4)
        dz = lax.rem((15 - step) // 4 + 2 + dx, 4)
        return dx, dz

    def target(step):
        dx, dz = offsets(step)
        return lax.rem(z_me + dz, 4) * 4 + lax.rem(x_me + dx, 4)

    def source(step):
        dx, dz = offsets(step)
        return lax.rem(z_me + 4 - dz, 4) * 4 + lax.rem(x_me + 4 - dx, 4)

    def copy_a(c, slot):
        return pltpu.make_async_remote_copy(
            src_ref=stage.at[c],
            dst_ref=xin.at[slot],
            send_sem=send_a.at[c],
            recv_sem=recv_a.at[slot],
            device_id=(c // NY, lax.rem(c, NY) * 2 + k_me),
            device_id_type=MESH,
        )

    def copy_d(c, slot):
        return pltpu.make_async_remote_copy(
            src_ref=outb.at[c],
            dst_ref=rin.at[slot],
            send_sem=send_d.at[c],
            recv_sem=recv_d.at[slot],
            device_id=(c // NY, lax.rem(c, NY) * 2 + k_me),
            device_id_type=MESH,
        )

    def send_all(step, carry):
        q = target(step)
        for dy in (2, 1, 3, 0):
            c = q * NY + lax.rem(y_me + dy, NY)

            @pl.when(c != c_me)
            def _():
                copy_a(c, c_me).start()

        return carry

    lax.fori_loop(0, NQ, send_all, 0)
    xin[c_me] = stage[c_me]

    both = jnp.where(lane < 64, side[0], side[1])
    names = jnp.zeros((32, 128), F32)
    for n in range(NBLK):
        row = memb[n // 2 : n // 2 + 1, :].astype(F32)
        other = pltpu.roll(row, 64, 1)
        row = jnp.where(lane < 64, row, other) if n % 2 == 0 else jnp.where(lane < 64, other, row)
        names = jnp.where(both == n, row, names)
    ids[...] = names


    loads[3].wait()
    count = jnp.zeros((1, 128), F32)
    for d in range(8):
        count = count + mask_ref[pp, d].astype(F32)
    share_of = jnp.concatenate([(1.0 / 32.0) / count] * 4, axis=1)

    def hilbert(value):
        for j in range(4):
            swapped = pltpu.roll(value[:, j * 128 : (j + 1) * 128], 64, 1)
            xst[j * 256 : (j + 1) * 256, :] = swapped.astype(BF16)
        part = [dot(band[:, (3 - t) * 256 : (7 - t) * 256], xst[...]) for t in range(4)]
        wrapped = [pltpu.roll(part[3], 16, 0)] + part
        return jnp.concatenate(
            [jnp.where(lane < 64, wrapped[j], wrapped[j + 1]) for j in range(4)], axis=1
        )

    loads[4].wait()

    def turn(a, carry):
        one = obsr[a].astype(F32)
        obst[pl.ds(pl.multiple_of(a * 128, 128), 128), :] = jnp.concatenate([one, one], axis=0).T
        return carry

    lax.fori_loop(0, 16, turn, 0)

    def place_lags(n, carry):
        for j in range(4):
            first = obst[pl.ds(n * 8 + 2 * j, 16, stride=128), :]
            second = obst[pl.ds(n * 8 + 2 * j + 1, 16, stride=128), :]
            obsf[pl.ds(pl.multiple_of(n * 16, 16), 16), j * 128 : (j + 1) * 128] = jnp.where(
                lane < 64, first, second
            )
        return carry

    lax.fori_loop(0, N1, place_lags, 0)
    loads[5].wait()
    obs_f = obsf[...]
    hil_o = hilbert(obs_f)
    envo[...] = jnp.sqrt(obs_f * obs_f + hil_o * hil_o)

    acc[...] = jnp.zeros_like(acc)
    loads[6].wait()

    amods, bmods = (amod_e, amod_o), (bmod_e, bmod_o)

    def rotate(step, slot, odd):
        q = source(step)
        for y in range(NY):
            c = q * NY + y

            @pl.when(c != c_me)
            def _():
                copy_a(c, c).wait_recv()

        amod, bmod = amods[odd], bmods[odd]
        for y in range(NY):
            x = xin[q * NY + y].astype(F32) * mask_ref[pp, 2 * y + k_me].astype(F32)
            xr = pltpu.roll(x, 64, 1)
            lanes = slice(y * 128, (y + 1) * 128)
            for h in range(2):
                rows = slice(h * 16, (h + 1) * 16)
                for n in range(N1):
                    turned = x[rows] * tab[q, CA + n : CA + n + 1, :]
                    turned = turned + xr[rows] * tab[q, SA + n : SA + n + 1, :]
                    amod[slot, h * 256 + n * 16 : h * 256 + (n + 1) * 16, lanes] = turned.astype(BF16)
            for n in range(N2):
                turned = x[32:] * tab[q, CB + n : CB + n + 1, :]
                turned = turned + xr[32:] * tab[q, SB + n : SB + n + 1, :]
                bmod[slot, n * 64 : (n + 1) * 64, lanes] = turned.astype(BF16)

    def correlate(slot, odd):
        acc[...] += lax.dot_general(
            amods[odd][slot],
            bmods[odd][slot],
            (((1,), (1,)), ((), ())),
            preferred_element_type=F32,
        ).reshape(2, 256, 512)

    rotate(0, 0, 0)

    def forward(i, carry):
        rotate(2 * i + 1, i, 1)
        correlate(i, 0)
        rotate(2 * i + 2, i + 1, 0)
        correlate(i, 1)
        return carry

    lax.fori_loop(0, NQ // 2 - 1, forward, 0)
    correlate(NQ // 2 - 1, 0)
    rotate(NQ - 1, NQ // 2 - 1, 1)
    rows_mine = pl.ds(pl.multiple_of(k_me * 256, 256), 256)
    rows_other = pl.ds(pl.multiple_of((1 - k_me) * 256, 256), 256)

    def last_half(rows):
        return lax.dot_general(
            amod_o[NQ // 2 - 1, rows, :],
            bmod_o[NQ // 2 - 1],
            (((1,), (1,)), ((), ())),
            preferred_element_type=F32,
        )

    def slot_of(step):
        dx, dz = offsets(step)
        dx, dz = lax.rem(4 - dx, 4), lax.rem(4 - dz, 4)
        return (15 - 4 * lax.rem(dz + 6 - dx, 4) - lax.rem(dx + 2, 4)) // 2

    acc_out[...] = (acc[1 - k_me] + last_half(rows_other)).astype(BF16)
    swap = pltpu.make_async_remote_copy(
        src_ref=acc_out,
        dst_ref=acc_in,
        send_sem=send_x.at[0],
        recv_sem=recv_x.at[0],
        device_id=partner,
        device_id_type=MESH,
    )
    swap.start()
    acc[k_me] += last_half(rows_mine)
    swap.wait_recv()
    stacked = (acc[k_me] + acc_in[...].astype(F32)) * share_of
    hil_s = hilbert(stacked)
    env_s = jnp.sqrt(stacked * stacked + hil_s * hil_s)
    residual = (stacked - obsf[...]) * (
        (1.0 + env_s) / (1.0 + env_s + envo[...])
    )
    rfull[k_me] = (residual * share_of).astype(BF16)
    share = pltpu.make_async_remote_copy(
        src_ref=rfull.at[k_me],
        dst_ref=rfull.at[k_me],
        send_sem=send_x.at[1],
        recv_sem=recv_x.at[1],
        device_id=partner,
        device_id_type=MESH,
    )
    share.start()
    rturn[k_me] = rfull[k_me].T
    first = slot_of(0)
    tbuf_e[rows_mine, :] = dot(rfull[k_me], bmod_e[first])
    ubuf_e[...] = dot(rturn[k_me], amod_e[first, rows_mine, :])
    pltpu.make_async_remote_copy(
        src_ref=rfull.at[1 - k_me],
        dst_ref=rfull.at[1 - k_me],
        send_sem=send_x.at[1],
        recv_sem=recv_x.at[1],
        device_id=partner,
        device_id_type=MESH,
    ).wait_recv()
    rturn[1 - k_me] = rfull[1 - k_me].T
    tbuf_e[rows_other, :] = dot(rfull[1 - k_me], bmod_e[first])
    ubuf_e[...] += dot(rturn[1 - k_me], amod_e[first, rows_other, :])

    tbufs, ubufs = (tbuf_e, tbuf_o), (ubuf_e, ubuf_o)

    def spread_a(step, odd):
        tbufs[odd][...] = dot(rfull[...].reshape(512, 512), bmods[odd][slot_of(step)])

    def spread_b(step, odd):
        turned = jnp.concatenate([rturn[0], rturn[1]], axis=1)
        ubufs[odd][...] = dot(turned, amods[odd][slot_of(step)])

    def unrotate(step, odd, days):
        q = target(step)
        tbuf, ubuf = tbufs[odd], ubufs[odd]
        for y in days:
            c = q * NY + y
            lanes = slice(y * 128, (y + 1) * 128)
            for h in range(2):
                straight = jnp.zeros((16, 128), F32)
                crossed = jnp.zeros((16, 128), F32)
                for n in range(N1):
                    t = tbuf[h * 256 + n * 16 : h * 256 + (n + 1) * 16, lanes]
                    straight = straight + t * tab[q, CA + n : CA + n + 1, :]
                    crossed = crossed + t * tab[q, SA + n : SA + n + 1, :]
                outb[c, h * 16 : (h + 1) * 16, :] = (
                    straight + pltpu.roll(crossed, 64, 1)
                ).astype(BF16)
            straight = jnp.zeros((64, 128), F32)
            crossed = jnp.zeros((64, 128), F32)
            for n in range(N2):
                u = ubuf[n * 64 : (n + 1) * 64, lanes]
                straight = straight + u * tab[q, CB + n : CB + n + 1, :]
                crossed = crossed + u * tab[q, SB + n : SB + n + 1, :]
            outb[c, 32:96, :] = (straight + pltpu.roll(crossed, 64, 1)).astype(BF16)

    def post(step):
        q = target(step)
        for dy in (2, 1, 3, 0):
            c = q * NY + lax.rem(y_me + dy, NY)

            @pl.when(c != c_me)
            def _():
                copy_d(c, c_me).start()

    def settle(step, copy_of):
        q = target(step)
        for y in range(NY):
            c = q * NY + y

            @pl.when(c != c_me)
            def _():
                copy_of(c, c_me).wait_send()

    def both_steps(step, odd):
        spread_a(step + 1, 1 - odd)
        unrotate(step, odd, (0, 1))
        spread_b(step + 1, 1 - odd)
        unrotate(step, odd, (2, 3))
        post(step)
        settle(step, copy_a)

    def adjoint(i, carry):
        both_steps(2 * i, 0)
        both_steps(2 * i + 1, 1)
        return carry

    lax.fori_loop(0, NQ // 2 - 1, adjoint, 0)
    both_steps(NQ - 2, 0)
    unrotate(NQ - 1, 1, range(NY))
    post(NQ - 1)
    settle(NQ - 1, copy_a)
    rin[c_me] = outb[c_me]

    out_ref[...] = jnp.zeros_like(out_ref)
    station = lax.broadcasted_iota(jnp.int32, (NSTA, 128), 0).astype(F32)
    blank = jnp.zeros((64, 128), BF16)

    def gather(step, carry):
        q = source(step)
        for y in range(NY):
            c = q * NY + y

            @pl.when(c != c_me)
            def _():
                copy_d(c, c).wait_recv()

        for half in range(2):
            c = q * NY + 2 * half
            place = (station == ids[pl.ds(2 * q + half, 1), :]).astype(F32).astype(BF16)
            rows = jnp.concatenate(
                [rin[c, 0:32, :], rin[c + 1, 0:32, :], rin[c, 32:96, :], blank, rin[c + 1, 32:96, :]],
                axis=0,
            )
            out_ref[...] += dot(jnp.concatenate([place, place], axis=1), rows)
        settle(step, copy_d)
        return carry

    lax.fori_loop(0, NQ, gather, 0)

    swap.wait_send()
    share.wait_send()


def body(spectra, observed, pair_blocks, members, day_mask):
    vm = pl.BlockSpec(memory_space=pltpu.VMEM)
    hbm = pl.BlockSpec(memory_space=pltpu.HBM)
    return pl.pallas_call(
        kernel,
        out_shape=jax.ShapeDtypeStruct((NSTA, 128), F32),
        in_specs=[hbm] * 7,
        out_specs=vm,
        scratch_shapes=[
            pltpu.SMEM((2, 8), jnp.int32),
            pltpu.VMEM((2, 32), jnp.int32),
            pltpu.VMEM((4, 128), jnp.int32),
            pltpu.VMEM((NSTA, 128), BF16),
            pltpu.VMEM((NSTA, 128), F32),
            pltpu.VMEM((2, 32, 128), F32),
            pltpu.VMEM((32, 128), F32),
            pltpu.VMEM((NC, ROWS, 128), BF16),
            pltpu.VMEM((NC, ROWS, 128), BF16),
            pltpu.VMEM((NQ // 2, 512, 512), BF16),
            pltpu.VMEM((NQ // 2, 512, 512), BF16),
            pltpu.VMEM((NQ // 2, 512, 512), BF16),
            pltpu.VMEM((NQ // 2, 512, 512), BF16),
            pltpu.VMEM((2, 256, 512), F32),
            pltpu.VMEM((256, 512), BF16),
            pltpu.VMEM((256, 512), BF16),
            pltpu.VMEM((16, B, L), BF16),
            pltpu.VMEM((16 * L, 128), F32),
            pltpu.VMEM((256, 512), F32),
            pltpu.VMEM((256, 512), F32),
            pltpu.VMEM((4 * 256, 128), BF16),
            pltpu.VMEM((NQ, 2 * (N1 + N2), 128), F32),
            pltpu.VMEM((256, 7 * 256), BF16),
            pltpu.VMEM((2, 256, 512), BF16),
            pltpu.VMEM((2, 512, 256), BF16),
            pltpu.VMEM((512, 512), F32),
            pltpu.VMEM((512, 512), F32),
            pltpu.VMEM((512, 512), F32),
            pltpu.VMEM((512, 512), F32),
            pltpu.VMEM((NC, ROWS, 128), BF16),
            pltpu.VMEM((NC, ROWS, 128), BF16),
            pltpu.SemaphoreType.DMA((NC,)),
            pltpu.SemaphoreType.DMA((NC,)),
            pltpu.SemaphoreType.DMA((NC,)),
            pltpu.SemaphoreType.DMA((NC,)),
            pltpu.SemaphoreType.DMA((2,)),
            pltpu.SemaphoreType.DMA((2,)),
            pltpu.SemaphoreType.DMA((7,)),
        ],
        compiler_params=pltpu.CompilerParams(
            collective_id=0, has_side_effects=True, vmem_limit_bytes=56000000
        ),
        name="stack_adjoint",
    )(
        *[
            pltpu.with_memory_space_constraint(value, pltpu.HBM)
            for value in (
                day_mask,
                pair_blocks.T,
                members.reshape(4, 128),
                spectra,
                observed,
                phase_tables(),
                hilbert_band(),
            )
        ],
    )[None]


def solution(mesh):
    return jax.shard_map(
        body,
        mesh=mesh,
        in_specs=(
            P("days", None, "pairs"),
            P("pairs", None, None, None),
            P(),
            P(),
            P("pairs", None),
        ),
        out_specs=P("days", None, "pairs"),
        check_vma=False,
    )
```

```python
import functools

import jax
import jax.numpy as jnp
import numpy as np
from jax import lax
from jax.experimental import pallas as pl
from jax.experimental.pallas import tpu as pltpu
from jax.sharding import PartitionSpec as P

B = 64
F = 1024
L = 128
NBLK = 8
NSTA = 512
N1 = 16
N2 = 8
NQ = 16
NY = 4
NC = NQ * NY
ROWS = 96
MESH = pl.DeviceIdType.MESH
F32 = jnp.float32
BF16 = jnp.bfloat16


def phase_tables():
    freq = 64 * np.arange(NQ)[:, None] + np.arange(128)[None, :] % 64
    sign = np.where(np.arange(128) < 64, -1.0, 1.0)[None, None, :]
    tables = []
    for shift in (N2 * np.arange(N1) - L // 2, -np.arange(N2)):
        turns = (freq[:, None, :] * shift[None, :, None]) % (2 * F)
        angle = np.pi * turns / F
        tables += [np.cos(angle), np.sin(angle) * sign]
    return np.concatenate(tables, axis=1).astype(np.float32)


CA, SA, CB, SB = 0, N1, 2 * N1, 2 * N1 + N2


def hilbert_band():
    blocks = []
    for k in range(7, -7, -2):
        offset = (8 * (np.arange(N1)[:, None] - np.arange(N1)[None, :]) + k) % L
        angle = np.pi * offset / L
        value = 2.0 / L * np.cos(angle) / np.sin(angle)
        blocks.append(np.kron(value, np.eye(16)))
    return np.concatenate(blocks, axis=1).astype(np.float32).astype(jnp.bfloat16)


def dot(a, b):
    return lax.dot_general(a, b, (((1,), (0,)), ((), ())), preferred_element_type=F32)


def kernel(
    mask_hbm, pb_hbm, memb_hbm, spec_hbm, obs_hbm, tab_hbm, band_hbm, out_ref,
    mask_ref, pb, memb, spec, sperm, side, ids,
    stage, xin, amod_e, amod_o, bmod_e, bmod_o, acc, acc_out, acc_in, obsr, obst, obsf, envo, xst, tab, band,
    rfull, rturn, tbuf_e, tbuf_o, ubuf_e, ubuf_o, outb, rin,
    send_a, recv_a, send_d, recv_d, send_x, recv_x, load,
):
    q_me = lax.axis_index("pairs")
    d_me = lax.axis_index("days")
    y_me = d_me // 2
    k_me = lax.rem(d_me, 2)
    c_me = q_me * NY + y_me
    z_me = q_me // 4
    x_me = lax.rem(q_me, 4)
    pp = y_me // 2
    partner = (q_me, y_me * 2 + 1 - k_me)

    barrier = pltpu.get_barrier_semaphore()

    row_a = lax.rem(y_me, 2) * 32 + k_me * 16
    loads = [
        pltpu.make_async_copy(memb_hbm, memb, load.at[0]),
        pltpu.make_async_copy(pb_hbm, pb, load.at[1]),
        pltpu.make_async_copy(spec_hbm.at[0], spec, load.at[2]),
        pltpu.make_async_copy(mask_hbm, mask_ref, load.at[3]),
        pltpu.make_async_copy(obs_hbm.at[pp, pl.ds(row_a, 16)], obsr, load.at[4]),
        pltpu.make_async_copy(band_hbm, band, load.at[5]),
        pltpu.make_async_copy(tab_hbm, tab, load.at[6]),
    ]
    for copy in loads:
        copy.start()

    def greet(c, carry):
        @pl.when(c != c_me)
        def _():
            pl.semaphore_signal(
                barrier, inc=1, device_id=(c // NY, lax.rem(c, NY) * 2 + k_me), device_id_type=MESH
            )

        return carry

    lax.fori_loop(0, NC, greet, 0)
    pl.semaphore_signal(barrier, inc=1, device_id=partner, device_id_type=MESH)

    lane = lax.broadcasted_iota(jnp.int32, (1, 128), 1)
    loads[0].wait()
    column = jnp.concatenate([memb[...], memb[...]], axis=0).astype(F32).T
    loads[1].wait()
    pair_col = jnp.concatenate([pb[...]] * 4, axis=0).astype(F32).T
    loads[2].wait()
    lane_s = lax.broadcasted_iota(jnp.int32, (128, NSTA), 1).astype(F32)
    for j in range(4):
        select = (lane_s == column[:, j : j + 1]).astype(F32).astype(BF16)
        sperm[j * 128 : (j + 1) * 128, :] = dot(select, spec[...])

    side[0] = jnp.broadcast_to(pair_col[:, 0:1], (32, 128))
    side[1] = jnp.broadcast_to(pair_col[:, 1:2], (32, 128))
    def fill(pair, carry):
        rows = []
        for t in range(2):
            block = side[t, pl.ds(pair, 1), :]
            picked = sperm[0:64, :]
            for n in range(1, NBLK):
                picked = jnp.where(block == n, sperm[n * 64 : (n + 1) * 64, :], picked)
            rows.append(picked.astype(BF16))
        for h in range(2):
            stage[2 * pair + h, 0:32, :] = rows[0][h * 32 : (h + 1) * 32]
            stage[2 * pair + h, 32:96, :] = rows[1]
        return carry

    lax.fori_loop(0, 32, fill, 0)
    pl.semaphore_wait(barrier, NC)

    def offsets(step):
        dx = lax.rem(17 - step, 4)
        dz = lax.rem((15 - step) // 4 + 2 + dx, 4)
        return dx, dz

    def target(step):
        dx, dz = offsets(step)
        return lax.rem(z_me + dz, 4) * 4 + lax.rem(x_me + dx, 4)

    def source(step):
        dx, dz = offsets(step)
        return lax.rem(z_me + 4 - dz, 4) * 4 + lax.rem(x_me + 4 - dx, 4)

    def copy_a(c, slot):
        return pltpu.make_async_remote_copy(
            src_ref=stage.at[c],
            dst_ref=xin.at[slot],
            send_sem=send_a.at[c],
            recv_sem=recv_a.at[slot],
            device_id=(c // NY, lax.rem(c, NY) * 2 + k_me),
            device_id_type=MESH,
        )

    def copy_d(c, slot):
        return pltpu.make_async_remote_copy(
            src_ref=outb.at[c],
            dst_ref=rin.at[slot],
            send_sem=send_d.at[c],
            recv_sem=recv_d.at[slot],
            device_id=(c // NY, lax.rem(c, NY) * 2 + k_me),
            device_id_type=MESH,
        )

    def send_all(step, carry):
        q = target(step)
        for dy in (2, 1, 3, 0):
            c = q * NY + lax.rem(y_me + dy, NY)

            @pl.when(c != c_me)
            def _():
                copy_a(c, c_me).start()

        return carry

    lax.fori_loop(0, NQ, send_all, 0)
    xin[c_me] = stage[c_me]

    both = jnp.where(lane < 64, side[0], side[1])
    names = jnp.zeros((32, 128), F32)
    for n in range(NBLK):
        row = memb[n // 2 : n // 2 + 1, :].astype(F32)
        other = pltpu.roll(row, 64, 1)
        row = jnp.where(lane < 64, row, other) if n % 2 == 0 else jnp.where(lane < 64, other, row)
        names = jnp.where(both == n, row, names)
    ids[...] = names


    loads[3].wait()
    count = jnp.zeros((1, 128), F32)
    for d in range(8):
        count = count + mask_ref[pp, d].astype(F32)
    share_of = jnp.concatenate([(1.0 / 32.0) / count] * 4, axis=1)

    def hilbert(value):
        for j in range(4):
            swapped = pltpu.roll(value[:, j * 128 : (j + 1) * 128], 64, 1)
            xst[j * 256 : (j + 1) * 256, :] = swapped.astype(BF16)
        part = [dot(band[:, (3 - t) * 256 : (7 - t) * 256], xst[...]) for t in range(4)]
        wrapped = [pltpu.roll(part[3], 16, 0)] + part
        return jnp.concatenate(
            [jnp.where(lane < 64, wrapped[j], wrapped[j + 1]) for j in range(4)], axis=1
        )

    loads[4].wait()

    def turn(a, carry):
        one = obsr[a].astype(F32)
        obst[pl.ds(pl.multiple_of(a * 128, 128), 128), :] = jnp.concatenate([one, one], axis=0).T
        return carry

    lax.fori_loop(0, 16, turn, 0)

    def place_lags(n, carry):
        for j in range(4):
            first = obst[pl.ds(n * 8 + 2 * j, 16, stride=128), :]
            second = obst[pl.ds(n * 8 + 2 * j + 1, 16, stride=128), :]
            obsf[pl.ds(pl.multiple_of(n * 16, 16), 16), j * 128 : (j + 1) * 128] = jnp.where(
                lane < 64, first, second
            )
        return carry

    lax.fori_loop(0, N1, place_lags, 0)
    loads[5].wait()
    obs_f = obsf[...]
    hil_o = hilbert(obs_f)
    envo[...] = jnp.sqrt(obs_f * obs_f + hil_o * hil_o)

    acc[...] = jnp.zeros_like(acc)
    loads[6].wait()

    amods, bmods = (amod_e, amod_o), (bmod_e, bmod_o)

    def rotate(step, slot, odd):
        q = source(step)
        for y in range(NY):
            c = q * NY + y

            @pl.when(c != c_me)
            def _():
                copy_a(c, c).wait_recv()

        amod, bmod = amods[odd], bmods[odd]
        for y in range(NY):
            x = xin[q * NY + y].astype(F32) * mask_ref[pp, 2 * y + k_me].astype(F32)
            xr = pltpu.roll(x, 64, 1)
            lanes = slice(y * 128, (y + 1) * 128)
            for h in range(2):
                rows = slice(h * 16, (h + 1) * 16)
                for n in range(N1):
                    turned = x[rows] * tab[q, CA + n : CA + n + 1, :]
                    turned = turned + xr[rows] * tab[q, SA + n : SA + n + 1, :]
                    amod[slot, h * 256 + n * 16 : h * 256 + (n + 1) * 16, lanes] = turned.astype(BF16)
            for n in range(N2):
                turned = x[32:] * tab[q, CB + n : CB + n + 1, :]
                turned = turned + xr[32:] * tab[q, SB + n : SB + n + 1, :]
                bmod[slot, n * 64 : (n + 1) * 64, lanes] = turned.astype(BF16)

    def correlate(slot, odd):
        acc[...] += lax.dot_general(
            amods[odd][slot],
            bmods[odd][slot],
            (((1,), (1,)), ((), ())),
            preferred_element_type=F32,
        ).reshape(2, 256, 512)

    rotate(0, 0, 0)

    def forward(i, carry):
        rotate(2 * i + 1, i, 1)
        correlate(i, 0)
        rotate(2 * i + 2, i + 1, 0)
        correlate(i, 1)
        return carry

    lax.fori_loop(0, NQ // 2 - 1, forward, 0)
    correlate(NQ // 2 - 1, 0)
    rotate(NQ - 1, NQ // 2 - 1, 1)
    rows_mine = pl.ds(pl.multiple_of(k_me * 256, 256), 256)
    rows_other = pl.ds(pl.multiple_of((1 - k_me) * 256, 256), 256)

    def last_half(rows):
        return lax.dot_general(
            amod_o[NQ // 2 - 1, rows, :],
            bmod_o[NQ // 2 - 1],
            (((1,), (1,)), ((), ())),
            preferred_element_type=F32,
        )

    def slot_of(step):
        dx, dz = offsets(step)
        dx, dz = lax.rem(4 - dx, 4), lax.rem(4 - dz, 4)
        return (15 - 4 * lax.rem(dz + 6 - dx, 4) - lax.rem(dx + 2, 4)) // 2

    acc_out[...] = (acc[1 - k_me] + last_half(rows_other)).astype(BF16)
    swap = pltpu.make_async_remote_copy(
        src_ref=acc_out,
        dst_ref=acc_in,
        send_sem=send_x.at[0],
        recv_sem=recv_x.at[0],
        device_id=partner,
        device_id_type=MESH,
    )
    swap.start()
    acc[k_me] += last_half(rows_mine)
    swap.wait_recv()
    stacked = (acc[k_me] + acc_in[...].astype(F32)) * share_of
    hil_s = hilbert(stacked)
    env_s = jnp.sqrt(stacked * stacked + hil_s * hil_s)
    residual = (stacked - obsf[...]) * (
        (1.0 + env_s) / (1.0 + env_s + envo[...])
    )
    rfull[k_me] = (residual * share_of).astype(BF16)
    share = pltpu.make_async_remote_copy(
        src_ref=rfull.at[k_me],
        dst_ref=rfull.at[k_me],
        send_sem=send_x.at[1],
        recv_sem=recv_x.at[1],
        device_id=partner,
        device_id_type=MESH,
    )
    share.start()
    rturn[k_me] = rfull[k_me].T
    first = slot_of(0)
    tbuf_e[rows_mine, :] = dot(rfull[k_me], bmod_e[first])
    ubuf_e[...] = dot(rturn[k_me], amod_e[first, rows_mine, :])
    pltpu.make_async_remote_copy(
        src_ref=rfull.at[1 - k_me],
        dst_ref=rfull.at[1 - k_me],
        send_sem=send_x.at[1],
        recv_sem=recv_x.at[1],
        device_id=partner,
        device_id_type=MESH,
    ).wait_recv()
    rturn[1 - k_me] = rfull[1 - k_me].T
    tbuf_e[rows_other, :] = dot(rfull[1 - k_me], bmod_e[first])
    ubuf_e[...] += dot(rturn[1 - k_me], amod_e[first, rows_other, :])

    tbufs, ubufs = (tbuf_e, tbuf_o), (ubuf_e, ubuf_o)

    def spread_a(step, odd):
        tbufs[odd][...] = dot(rfull[...].reshape(512, 512), bmods[odd][slot_of(step)])

    def spread_b(step, odd):
        turned = jnp.concatenate([rturn[0], rturn[1]], axis=1)
        ubufs[odd][...] = dot(turned, amods[odd][slot_of(step)])

    def unrotate(step, odd, days):
        q = target(step)
        tbuf, ubuf = tbufs[odd], ubufs[odd]
        for y in days:
            c = q * NY + y
            lanes = slice(y * 128, (y + 1) * 128)
            for h in range(2):
                straight = jnp.zeros((16, 128), F32)
                crossed = jnp.zeros((16, 128), F32)
                for n in range(N1):
                    t = tbuf[h * 256 + n * 16 : h * 256 + (n + 1) * 16, lanes]
                    straight = straight + t * tab[q, CA + n : CA + n + 1, :]
                    crossed = crossed + t * tab[q, SA + n : SA + n + 1, :]
                outb[c, h * 16 : (h + 1) * 16, :] = (
                    straight + pltpu.roll(crossed, 64, 1)
                ).astype(BF16)
            straight = jnp.zeros((64, 128), F32)
            crossed = jnp.zeros((64, 128), F32)
            for n in range(N2):
                u = ubuf[n * 64 : (n + 1) * 64, lanes]
                straight = straight + u * tab[q, CB + n : CB + n + 1, :]
                crossed = crossed + u * tab[q, SB + n : SB + n + 1, :]
            outb[c, 32:96, :] = (straight + pltpu.roll(crossed, 64, 1)).astype(BF16)

    def post(step):
        q = target(step)
        for dy in (2, 1, 3, 0):
            c = q * NY + lax.rem(y_me + dy, NY)

            @pl.when(c != c_me)
            def _():
                copy_d(c, c_me).start()

    def settle(step, copy_of):
        q = target(step)
        for y in range(NY):
            c = q * NY + y

            @pl.when(c != c_me)
            def _():
                copy_of(c, c_me).wait_send()

    def both_steps(step, odd):
        spread_a(step + 1, 1 - odd)
        unrotate(step, odd, (0, 1))
        spread_b(step + 1, 1 - odd)
        unrotate(step, odd, (2, 3))
        post(step)
        settle(step, copy_a)

    def adjoint(i, carry):
        both_steps(2 * i, 0)
        both_steps(2 * i + 1, 1)
        return carry

    lax.fori_loop(0, NQ // 2 - 1, adjoint, 0)
    both_steps(NQ - 2, 0)
    unrotate(NQ - 1, 1, range(NY))
    post(NQ - 1)
    settle(NQ - 1, copy_a)
    rin[c_me] = outb[c_me]

    out_ref[...] = jnp.zeros_like(out_ref)
    station = lax.broadcasted_iota(jnp.int32, (NSTA, 128), 0).astype(F32)
    blank = jnp.zeros((64, 128), BF16)

    def gather(step, carry):
        q = source(step)
        for y in range(NY):
            c = q * NY + y

            @pl.when(c != c_me)
            def _():
                copy_d(c, c).wait_recv()

        for half in range(2):
            c = q * NY + 2 * half
            place = (station == ids[pl.ds(2 * q + half, 1), :]).astype(F32).astype(BF16)
            rows = jnp.concatenate(
                [rin[c, 0:32, :], rin[c + 1, 0:32, :], rin[c, 32:96, :], blank, rin[c + 1, 32:96, :]],
                axis=0,
            )
            out_ref[...] += dot(jnp.concatenate([place, place], axis=1), rows)
        settle(step, copy_d)
        return carry

    lax.fori_loop(0, NQ, gather, 0)

    swap.wait_send()
    share.wait_send()


def body(spectra, observed, pair_blocks, members, day_mask):
    vm = pl.BlockSpec(memory_space=pltpu.VMEM)
    hbm = pl.BlockSpec(memory_space=pltpu.HBM)
    return pl.pallas_call(
        kernel,
        out_shape=jax.ShapeDtypeStruct((NSTA, 128), F32),
        in_specs=[hbm] * 7,
        out_specs=vm,
        scratch_shapes=[
            pltpu.SMEM((2, 8), jnp.int32),
            pltpu.VMEM((2, 32), jnp.int32),
            pltpu.VMEM((4, 128), jnp.int32),
            pltpu.VMEM((NSTA, 128), BF16),
            pltpu.VMEM((NSTA, 128), F32),
            pltpu.VMEM((2, 32, 128), F32),
            pltpu.VMEM((32, 128), F32),
            pltpu.VMEM((NC, ROWS, 128), BF16),
            pltpu.VMEM((NC, ROWS, 128), BF16),
            pltpu.VMEM((NQ // 2, 512, 512), BF16),
            pltpu.VMEM((NQ // 2, 512, 512), BF16),
            pltpu.VMEM((NQ // 2, 512, 512), BF16),
            pltpu.VMEM((NQ // 2, 512, 512), BF16),
            pltpu.VMEM((2, 256, 512), F32),
            pltpu.VMEM((256, 512), BF16),
            pltpu.VMEM((256, 512), BF16),
            pltpu.VMEM((16, B, L), BF16),
            pltpu.VMEM((17 * L, 128), F32),
            pltpu.VMEM((256, 512), F32),
            pltpu.VMEM((256, 512), F32),
            pltpu.VMEM((4 * 256, 128), BF16),
            pltpu.VMEM((NQ, 2 * (N1 + N2), 128), F32),
            pltpu.VMEM((256, 7 * 256), BF16),
            pltpu.VMEM((2, 256, 512), BF16),
            pltpu.VMEM((2, 512, 256), BF16),
            pltpu.VMEM((512, 512), F32),
            pltpu.VMEM((512, 512), F32),
            pltpu.VMEM((512, 512), F32),
            pltpu.VMEM((512, 512), F32),
            pltpu.VMEM((NC, ROWS, 128), BF16),
            pltpu.VMEM((NC, ROWS, 128), BF16),
            pltpu.SemaphoreType.DMA((NC,)),
            pltpu.SemaphoreType.DMA((NC,)),
            pltpu.SemaphoreType.DMA((NC,)),
            pltpu.SemaphoreType.DMA((NC,)),
            pltpu.SemaphoreType.DMA((2,)),
            pltpu.SemaphoreType.DMA((2,)),
            pltpu.SemaphoreType.DMA((7,)),
        ],
        compiler_params=pltpu.CompilerParams(
            collective_id=0, has_side_effects=True, vmem_limit_bytes=56000000
        ),
        name="stack_adjoint",
    )(
        *[
            pltpu.with_memory_space_constraint(value, pltpu.HBM)
            for value in (
                day_mask,
                pair_blocks.T,
                members.reshape(4, 128),
                spectra,
                observed,
                phase_tables(),
                hilbert_band(),
            )
        ],
    )[None]


def solution(mesh):
    return jax.shard_map(
        body,
        mesh=mesh,
        in_specs=(
            P("days", None, "pairs"),
            P("pairs", None, None, None),
            P(),
            P(),
            P("pairs", None),
        ),
        out_specs=P("days", None, "pairs"),
        check_vma=False,
    )
```
